32 devices in a mesh: tm: 4 (over x, core), fibre: 8 (over z, y).
Axes of the slice: x: 2, y: 2, z: 4, core: 2. Of those that a mesh axis runs over, the one named last changes fastest.
Arguments:
- signal: float32 [64, 64, 1024], P(None, 'fibre', 'tm'), may hold values from -6 to 6
- first_kernel_weight: float32 [3, 3, 128, 64], replicated, may hold values from -0.25 to 0.25
- first_layer_bias: float32 [128], replicated, may hold values from -1 to 1
- first_residual_matrix: float32 [64, 64], replicated, may hold values from -0.75 to 0.75
- second_kernel_weight: float32 [3, 3, 128, 64], replicated, may hold values from -0.25 to 0.25
- second_layer_bias: float32 [128], replicated, may hold values from -1 to 1
- second_residual_matrix: float32 [64, 64], replicated, may hold values from -0.75 to 0.75
Outputs:
- features: float32 [64, 64, 1024], P(None, 'fibre', 'tm')
The draws below stay inside these ranges and needn't reach their ends.
All inputs are finite; a program needn't handle non-finite values.
Results may differ from the reference program's by a relative error of at most 0.0001.
Values sent between devices are 32-bit elements; how exact they have to be, the bound alone decides.
A program may use at most 64 MiB of HBM per device.

```python
import jax
import jax.numpy as jnp
from jax import lax

CH = 64
DILATION_ONE = 128
DILATION_TWO = 256
FIB_DEV = 8
FIBRES = 64
TIME = 1024


def level_of(stream_key, dims, cuts, least, top_value):
    level = 1.0
    for position, shards_of in cuts:
        heights = jax.random.uniform(jax.random.fold_in(jax.random.fold_in(stream_key, 6), position), (shards_of,), jnp.float32, least / len(cuts), top_value / len(cuts))
        level = level * jnp.repeat(jnp.exp(heights), dims[position] // shards_of).reshape((-1,) + (1,) * (len(dims) - 1 - position))
    return level


def bell_draw(key, dims, scale, most, split=(), kind=jnp.bfloat16):
    values = jax.random.normal(key, dims, jnp.float32) * scale
    if len(split) > 0:
        values = level_of(key, dims, split, -0.22, 0.18) * values
    return jnp.clip(values, min=-most, max=most).astype(kind)


def setup_inputs(seed: int = 0) -> dict:
    arg_keys = jax.random.split(jax.random.key(seed), 8)
    return {
        "signal": bell_draw(arg_keys[0], (CH, FIBRES, TIME), 1.0, 6.0, ((1, 8), (2, 4)), jnp.float32),
        "first_kernel_weight": bell_draw(arg_keys[1], (3, 3, 2 * CH, CH), (9 * CH) ** -0.5, 0.25, (), jnp.float32),
        "first_layer_bias": jnp.clip(jax.random.uniform(arg_keys[2], (2 * CH,), jnp.float32, -1.0, 1.0), -1.0, 1.0),
        "first_residual_matrix": bell_draw(arg_keys[3], (CH, CH), CH ** -0.5, 0.75, (), jnp.float32),
        "second_kernel_weight": bell_draw(arg_keys[4], (3, 3, 2 * CH, CH), (9 * CH) ** -0.5, 0.25, (), jnp.float32),
        "second_layer_bias": jnp.clip(jax.random.uniform(arg_keys[5], (2 * CH,), jnp.float32, -1.0, 1.0), -1.0, 1.0),
        "second_residual_matrix": bell_draw(arg_keys[6], (CH, CH), CH ** -0.5, 0.75, (), jnp.float32),
    }


def apply_gated_layer(widened_input, weight, bias, mixing, dilation):
    fibre_out = widened_input.shape[1] - 2
    time_out = widened_input.shape[2] - 2 * dilation
    preact = jnp.zeros((weight.shape[2], fibre_out, time_out), jnp.float32) + bias[:, None, None]
    for across in range(3):
        for along in range(3):
            offset = 2 * dilation - along * dilation
            window = widened_input[:, across:across + fibre_out, offset:offset + time_out]
            preact = preact + jnp.einsum("oc,cft->oft", weight[across, along], window, precision=lax.Precision.HIGHEST)
    channels = mixing.shape[0]
    gated = jnp.tanh(preact[:channels]) * jax.nn.sigmoid(preact[channels:])
    return widened_input[:, 1:-1, 2 * dilation:] + jnp.einsum("oc,cft->oft", mixing, gated, precision=lax.Precision.HIGHEST)


def complete_layer_output(field, weight, bias, mixing, dilation):
    padded = jnp.pad(field, ((0, 0), (1, 1), (2 * dilation, 0)))
    block_count = field.shape[1] // FIB_DEV

    def one_block(block_index):
        widened_input = lax.dynamic_slice_in_dim(padded, block_index * FIB_DEV, FIB_DEV + 2, 1)
        return apply_gated_layer(widened_input, weight, bias, mixing, dilation)

    blocks = lax.map(one_block, jnp.arange(block_count, dtype=jnp.int32))
    return jnp.transpose(blocks, (1, 0, 2, 3)).reshape(field.shape)


def reference(signal, first_kernel_weight, first_layer_bias, first_residual_matrix, second_kernel_weight, second_layer_bias, second_residual_matrix):
    between_layers = complete_layer_output(signal, first_kernel_weight, first_layer_bias, first_residual_matrix, DILATION_ONE)
    return complete_layer_output(between_layers, second_kernel_weight, second_layer_bias, second_residual_matrix, DILATION_TWO)
```

```python
import jax
import jax.numpy as jnp
from jax import lax
from jax.experimental import pallas as pl
from jax.experimental.pallas import tpu as pltpu
from jax.sharding import PartitionSpec as P

DILATION_ONE = 128
DILATION_TWO = 256
BF = jnp.bfloat16
F32 = jnp.float32


def split(value):
    hi = value.astype(BF)
    return hi, (value - hi.astype(F32)).astype(BF)


def thirds(value):
    hi, lo = split(value)
    return [hi, lo, hi]


def kernel(
    nt, nf, fib,
    x_hbm, w1_hbm, b1_hbm, r1_hbm, w2_hbm, b2_hbm, r2_hbm, out_ref,
    s, m, w1, b1, r1, w2, b2, r2, l1, l2, q1, q2, c1, c2, aa, bb,
    in_sem, w_sem, h0s, h0r, xs, xr, h2s, h2r, ps, pr, ts, tr, ms, mr, es, er,
):
    T = lax.axis_index("tm")
    F = lax.axis_index("fibre")
    odd = lax.rem(T, 2)
    even = odd == 0
    isodd = odd == 1
    partner = T + 1 - 2 * odd
    ch = x_hbm.shape[1]
    wide = fib + 4
    mid = fib + 2
    out_ch = 2 * ch
    far = nt > 4
    up, down = F + 1 < nf, F > 0

    def dev(t, f):
        return {"tm": t, "fibre": f}

    ins = [
        pltpu.make_async_copy(x_hbm.at[f], s.at[0, f + 2], in_sem.at[f]) for f in range(fib)
    ]
    for c in ins:
        c.start()
    weights = [
        pltpu.make_async_copy(a, b, w_sem.at[i])
        for i, (a, b) in enumerate(
            [(w1_hbm, w1), (b1_hbm, b1), (r1_hbm, r1), (w2_hbm, w2), (b2_hbm, b2), (r2_hbm, r2)]
        )
    ]
    for c in weights:
        c.start()

    barrier = pltpu.get_barrier_semaphore()
    friends = [(partner, F, None), (T, F + 1, up), (T, F - 1, down), (T + 2, F, T + 2 < nt), (T - 2, F, T >= 2)]
    if far:
        send3 = isodd & (T + 3 < nt)
        recv3 = even & (T >= 4)
        for e, ok in ((0, None), (1, up), (-1, down)):
            for d, okt in ((3, send3), (-3, recv3)):
                friends.append((T + d, F + e, okt if ok is None else okt & ok))
    count = jnp.int32(0)
    for t, f, ok in friends:
        if ok is None:
            pl.semaphore_signal(barrier, inc=1, device_id=dev(t, f), device_id_type=pl.DeviceIdType.MESH)
            count = count + 1
        else:
            @pl.when(ok)
            def _(t=t, f=f):
                pl.semaphore_signal(barrier, inc=1, device_id=dev(t, f), device_id_type=pl.DeviceIdType.MESH)
            count = count + ok.astype(jnp.int32)
    pl.semaphore_wait(barrier, count)

    def remote(src, dst, ssem, rsem, t, f):
        return pltpu.make_async_remote_copy(
            src_ref=src, dst_ref=dst, send_sem=ssem, recv_sem=rsem,
            device_id=dev(t, f), device_id_type=pl.DeviceIdType.MESH,
        )

    def halo_up(j, ss, rr):
        return remote(s.at[j, pl.ds(fib, 2)], s.at[j, pl.ds(0, 2)], ss.at[0], rr.at[0], T, F + 1)

    def halo_down(j, ss, rr):
        return remote(s.at[j, pl.ds(2, 2)], s.at[j, pl.ds(fib + 2, 2)], ss.at[1], rr.at[1], T, F - 1)

    def cross(f):
        return remote(x_hbm.at[f], s.at[2, f + 2], xs.at[f], xr.at[f], T + 2, F)

    order = [0, 1, fib - 2, fib - 1] + list(range(2, fib - 2))

    @pl.when(T + 2 < nt)
    def _():
        for f in order:
            cross(f).start()

    for f in (0, 1, fib - 2, fib - 1):
        ins[f].wait()

    @pl.when(up)
    def _():
        halo_up(0, h0s, h0r).start()

    @pl.when(down)
    def _():
        halo_down(0, h0s, h0r).start()

    if far:
        def third(i, e):
            if e == 0:
                src, dst = x_hbm, s.at[3, pl.ds(2, fib)]
            elif e == 1:
                src, dst = x_hbm.at[pl.ds(fib - 2, 2)], s.at[3, pl.ds(0, 2)]
            else:
                src, dst = x_hbm.at[pl.ds(0, 2)], s.at[3, pl.ds(fib + 2, 2)]
            return remote(src, dst, es.at[i], er.at[i], T + 3, F + e)

        thirds_list = [(0, 0, None, None), (1, 1, up, down), (2, -1, down, up)]
        for i, e, ok, _ok in thirds_list:
            @pl.when(send3 if ok is None else send3 & ok)
            def _(i=i, e=e):
                third(i, e).start()

    zero2 = jnp.zeros((2,) + s.shape[2:], F32)

    def zero_halo(j):
        @pl.when(jnp.logical_not(down))
        def _():
            s[j, pl.ds(0, 2)] = zero2

        @pl.when(jnp.logical_not(up))
        def _():
            s[j, pl.ds(fib + 2, 2)] = zero2

    zero_halo(0)

    @pl.when(T >= 2)
    def _():
        zero_halo(2)

    @pl.when(T == 0)
    def _():
        s[1] = jnp.zeros(s.shape[1:], F32)
        m[1] = jnp.zeros(m.shape[1:], F32)

    @pl.when(T < 2)
    def _():
        m[2] = jnp.zeros(m.shape[1:], F32)

    @pl.when(T == 2)
    def _():
        s[3] = jnp.zeros(s.shape[1:], F32)

    if far:
        @pl.when(recv3)
        def _():
            zero_halo(3)

    for f in range(2, fib - 2):
        ins[f].wait()
    for c in weights:
        c.wait()

    def prepare(w, left, r, mix, bias, tall):
        for a in range(3):
            for k in range(3):
                hi, lo = split(w[a, k])
                for i, piece in enumerate((hi, hi, lo)):
                    left[pl.ds(a * out_ch, out_ch), pl.ds((3 * k + i) * ch, ch)] = piece
        hi, lo = split(r[...])
        for i, piece in enumerate((hi, hi, lo)):
            mix[:, pl.ds(i * ch, ch)] = piece
        tall[...] = jnp.broadcast_to(bias[...], (out_ch, out_ch)).T

    prepare(w1, l1, r1, q1, b1, c1)
    prepare(w2, l2, r2, q2, b2, c2)

    def wait_halos(j, ss, rr):
        @pl.when(down)
        def _():
            halo_up(j, ss, rr).wait_recv()

        @pl.when(up)
        def _():
            halo_down(j, ss, rr).wait_recv()

    def push(slot, g, left, pieces):
        right = jnp.concatenate(pieces, axis=0)
        p = jnp.dot(left[...], right, preferred_element_type=F32)
        total = bb[slot] + p[2 * out_ch:]
        bb[slot] = aa[slot] + p[out_ch:2 * out_ch]
        aa[slot] = p[:out_ch]
        return total

    def gate(total, mix, tall, base):
        bias = tall[...]
        bias = jnp.concatenate([bias] * (total.shape[1] // bias.shape[1]), axis=1)
        pre = total + bias
        g = jnp.tanh(pre[:ch]) * (0.5 * jnp.tanh(0.5 * pre[ch:]) + 0.5)
        return base + jnp.dot(mix[...], jnp.concatenate(thirds(g), axis=0), preferred_element_type=F32)

    def first(slot, g, cur, prev, dst):
        chi, clo = split(s[cur, g])
        phi, plo = split(s[prev, g])
        d = DILATION_ONE
        shi = jnp.concatenate([phi[:, d:], chi[:, :d]], axis=1)
        slo = jnp.concatenate([plo[:, d:], clo[:, :d]], axis=1)
        total = push(slot, g, l1, [chi, clo, chi, shi, slo, shi, phi, plo, phi])

        @pl.when(g >= 2)
        def _():
            h = g - 2
            value = gate(total, q1, c1, s[cur, g - 1])
            row = F * fib + h - 1
            ok = (row >= 0) & (row < nf * fib)
            m[dst, h] = jnp.where(ok, value, 0.0)

    aa[...] = jnp.zeros_like(aa)
    bb[...] = jnp.zeros_like(bb)

    def part(src, g):
        return remote(s.at[src, g], s.at[1, g], ps.at[g], pr.at[g], partner, F)

    def part3(g):
        return remote(s.at[2, g], s.at[3, g], ts.at[g], tr.at[g], partner, F)

    def share(src, h):
        return remote(m.at[src, h], m.at[1, h], ms.at[h], mr.at[h], partner, F)

    wait_halos(0, h0s, h0r)

    @pl.when(even)
    def _():
        for g in range(wide):
            part(0, g).start()

    @pl.when(T >= 2)
    def _():
        for f in (0, 1, fib - 2, fib - 1):
            cross(f).wait_recv()

        @pl.when(up)
        def _():
            halo_up(2, h2s, h2r).start()

        @pl.when(down)
        def _():
            halo_down(2, h2s, h2r).start()

        wait_halos(2, h2s, h2r)

    if far:
        for i, e, _ok, ok in thirds_list:
            @pl.when(recv3 if ok is None else recv3 & ok)
            def _(i=i, e=e):
                third(i, e).wait_recv()

    def send_mid(h):
        @pl.when(even)
        def _():
            share(0, h).start()

        @pl.when(isodd & (T >= 2))
        def _():
            share(2, h).start()

    def step(g, carry):
        @pl.when(T >= 2)
        def _():
            @pl.when((g >= 4) & (g < fib))
            def _():
                cross(g - 2).wait_recv()

            @pl.when(even)
            def _():
                part3(g).start()

            @pl.when(isodd)
            def _():
                part(2, g).start()
                part3(g).wait_recv()

            first(1, g, 2, 3, 2)

        @pl.when(T >= 1)
        def _():
            part(0, g).wait_recv()

        first(0, g, 0, 1, 0)

        @pl.when(g >= 3)
        def _():
            send_mid(g - 3)
        return carry

    lax.fori_loop(0, wide, step, 0)
    send_mid(mid - 1)

    aa[...] = jnp.zeros_like(aa)
    bb[...] = jnp.zeros_like(bb)

    def last(h, carry):
        @pl.when(T >= 1)
        def _():
            share(0, h).wait_recv()
        pieces = []
        for k in range(3):
            pieces += thirds(m[k, h])
        total = push(0, h, l2, pieces)

        @pl.when(h >= 2)
        def _():
            out_ref[h - 2] = gate(total, q2, c2, m[0, h - 1])
        return carry

    lax.fori_loop(0, mid, last, 0)

    @pl.when(T + 2 < nt)
    def _():
        for f in range(fib):
            cross(f).wait_send()

    @pl.when(up)
    def _():
        halo_up(0, h0s, h0r).wait_send()

        @pl.when(T >= 2)
        def _():
            halo_up(2, h2s, h2r).wait_send()

    @pl.when(down)
    def _():
        halo_down(0, h0s, h0r).wait_send()

        @pl.when(T >= 2)
        def _():
            halo_down(2, h2s, h2r).wait_send()

    def drain(g, carry):
        @pl.when(even | (T >= 2))
        def _():
            part(0, g).wait_send()

        @pl.when(even & (T >= 2))
        def _():
            part3(g).wait_send()
        return carry

    lax.fori_loop(0, wide, drain, 0)

    @pl.when(even | (T >= 2))
    def _():
        for h in range(mid):
            share(0, h).wait_send()

    if far:
        for i, e, ok, _ok in thirds_list:
            @pl.when(send3 if ok is None else send3 & ok)
            def _(i=i, e=e):
                third(i, e).wait_send()


def solution(mesh):
    nt, nf = mesh.shape["tm"], mesh.shape["fibre"]
    placed = (P(None, "fibre", "tm"), P(), P(), P(), P(), P(), P())

    def body(signal, w1, b1, r1, w2, b2, r2):
        ch, fib, length = signal.shape
        assert length == DILATION_TWO == 2 * DILATION_ONE and nt % 2 == 0 and fib >= 4
        x = jnp.transpose(signal, (1, 0, 2))
        out_ch = w1.shape[2]
        b1 = b1.reshape(1, out_ch)
        b2 = b2.reshape(1, out_ch)
        dma = lambda n: pltpu.SemaphoreType.DMA((n,))
        out = pl.pallas_call(
            lambda *refs: kernel(nt, nf, fib, *refs),
            name="gated_layers",
            out_shape=jax.ShapeDtypeStruct((fib, ch, length), F32),
            in_specs=[pl.BlockSpec(memory_space=pl.ANY)] * 7,
            out_specs=pl.BlockSpec(memory_space=pltpu.VMEM),
            scratch_shapes=[
                pltpu.VMEM((4, fib + 4, ch, length), F32),
                pltpu.VMEM((3, fib + 2, ch, length), F32),
                pltpu.VMEM(w1.shape, F32), pltpu.VMEM(b1.shape, F32), pltpu.VMEM(r1.shape, F32),
                pltpu.VMEM(w2.shape, F32), pltpu.VMEM(b2.shape, F32), pltpu.VMEM(r2.shape, F32),
                pltpu.VMEM((3 * out_ch, 9 * ch), BF), pltpu.VMEM((3 * out_ch, 9 * ch), BF),
                pltpu.VMEM((ch, 3 * ch), BF), pltpu.VMEM((ch, 3 * ch), BF),
                pltpu.VMEM((out_ch, out_ch), F32), pltpu.VMEM((out_ch, out_ch), F32),
                pltpu.VMEM((2, out_ch, length), F32), pltpu.VMEM((2, out_ch, length), F32),
                dma(fib), dma(6), dma(2), dma(2), dma(fib), dma(fib), dma(2), dma(2),
                dma(fib + 4), dma(fib + 4), dma(fib + 4), dma(fib + 4),
                dma(fib + 2), dma(fib + 2), dma(3), dma(3),
            ],
            compiler_params=pltpu.CompilerParams(collective_id=0, has_side_effects=True),
        )(x, w1, b1, r1, w2, b2, r2)
        return jnp.transpose(out, (1, 0, 2))

    return jax.shard_map(body, mesh=mesh, in_specs=placed, out_specs=P(None, "fibre", "tm"), check_vma=False)
```

```python
import jax
import jax.numpy as jnp
from jax import lax
from jax.experimental import pallas as pl
from jax.experimental.pallas import tpu as pltpu
from jax.sharding import PartitionSpec as P

DILATION_ONE = 128
DILATION_TWO = 256
BF = jnp.bfloat16
F32 = jnp.float32


def split(value):
    hi = value.astype(BF)
    return hi, (value - hi.astype(F32)).astype(BF)


def thirds(value):
    hi, lo = split(value)
    return [hi, lo, hi]


def pick(i, values):
    out = jnp.int32(values[-1])
    for n in range(len(values) - 2, -1, -1):
        out = jnp.where(i == n, jnp.int32(values[n]), out)
    return out


def kernel(
    nt, nf, fib,
    x_hbm, w1_hbm, b1_hbm, r1_hbm, w2_hbm, b2_hbm, r2_hbm, out_ref,
    s, m, xv, w1, b1, r1, w2, b2, r2, l1, l2, q1, q2, c1, c2, acc, acc2,
    in_sem, w_sem, h0s, h0r, xs, xr, h2s, h2r, ps, pr, ts, tr, ms, mr, es, er,
):
    T = lax.axis_index("tm")
    F = lax.axis_index("fibre")
    odd = lax.rem(T, 2)
    even = odd == 0
    isodd = odd == 1
    late = T >= 2
    partner = T + 1 - 2 * odd
    ch, length = s.shape[2], s.shape[3] // 2
    own = fib // 2
    wide = own + 2
    mid = own + 1
    out_ch = 2 * ch
    far = nt > 4
    up, down = F + 1 < nf, F > 0
    arrive = [own] + list(range(1, own))
    order = [own, 0, 1, own + 1] + list(range(2, own))
    emits = [0, 0, 0, own] + list(range(1, own - 1))
    order2 = [0, own] + list(range(1, own))

    def dev(t, f):
        return {"tm": t, "fibre": f}

    load = pltpu.make_async_copy(x_hbm, xv, in_sem.at[0])
    load.start()
    weights = [
        pltpu.make_async_copy(a, b, w_sem.at[i])
        for i, (a, b) in enumerate(
            [(w1_hbm, w1), (b1_hbm, b1), (r1_hbm, r1), (w2_hbm, w2), (b2_hbm, b2), (r2_hbm, r2)]
        )
    ]
    for c in weights:
        c.start()

    barrier = pltpu.get_barrier_semaphore()
    friends = [(partner, F, None), (T, F + 1, up), (T, F - 1, down), (T + 2, F, T + 2 < nt), (T - 2, F, late)]
    if far:
        send3 = isodd & (T + 3 < nt)
        recv3 = even & (T >= 4)
        for e, ok in ((0, None), (1, up), (-1, down)):
            for d, okt in ((3, send3), (-3, recv3)):
                friends.append((T + d, F + e, okt if ok is None else okt & ok))
    count = jnp.int32(0)
    for t, f, ok in friends:
        if ok is None:
            pl.semaphore_signal(barrier, inc=1, device_id=dev(t, f), device_id_type=pl.DeviceIdType.MESH)
            count = count + 1
        else:
            @pl.when(ok)
            def _(t=t, f=f):
                pl.semaphore_signal(barrier, inc=1, device_id=dev(t, f), device_id_type=pl.DeviceIdType.MESH)
            count = count + ok.astype(jnp.int32)

    load.wait()
    for f in range(fib):
        for c in range(0, length, 128):
            s[0, 1 + f // 2, :, pl.ds((f % 2) * length + c, 128)] = xv[pl.ds(c // 128 * fib + f, ch, stride=fib * length // 128), :]
    pl.semaphore_wait(barrier, count)

    def remote(src, dst, ssem, rsem, t, f):
        return pltpu.make_async_remote_copy(
            src_ref=src, dst_ref=dst, send_sem=ssem, recv_sem=rsem,
            device_id=dev(t, f), device_id_type=pl.DeviceIdType.MESH,
        )

    def halo_up(j, ss, rr):
        return remote(s.at[j, own], s.at[j, 0], ss.at[0], rr.at[0], T, F + 1)

    def halo_down(j, ss, rr):
        return remote(s.at[j, 1], s.at[j, own + 1], ss.at[1], rr.at[1], T, F - 1)

    def cross(q):
        return remote(s.at[0, q], s.at[2, q], xs.at[q], xr.at[q], T + 2, F)

    @pl.when(T + 2 < nt)
    def _():
        for q in arrive:
            cross(q).start()

    @pl.when(up)
    def _():
        halo_up(0, h0s, h0r).start()

    @pl.when(down)
    def _():
        halo_down(0, h0s, h0r).start()

    def part(src, q):
        return remote(s.at[src, q], s.at[1, q], ps.at[q], pr.at[q], partner, F)

    def part3(q):
        return remote(s.at[2, q], s.at[3, q], ts.at[q], tr.at[q], partner, F)

    def share(src, r):
        return remote(m.at[src, r], m.at[1, r], ms.at[r], mr.at[r], partner, F)

    @pl.when(even)
    def _():
        for q in range(1, own + 1):
            part(0, q).start()

    if far:
        def third(i, e):
            if e == 0:
                src, dst = s.at[0, pl.ds(1, own)], s.at[3, pl.ds(1, own)]
            elif e == 1:
                src, dst = s.at[0, own], s.at[3, 0]
            else:
                src, dst = s.at[0, 1], s.at[3, own + 1]
            return remote(src, dst, es.at[i], er.at[i], T + 3, F + e)

        thirds_list = [(0, 0, None, None), (1, 1, up, down), (2, -1, down, up)]
        for i, e, ok, _ok in thirds_list:
            @pl.when(send3 if ok is None else send3 & ok)
            def _(i=i, e=e):
                third(i, e).start()

    zero = jnp.zeros(s.shape[2:], F32)

    def zero_halo(j):
        @pl.when(jnp.logical_not(down))
        def _():
            s[j, 0] = zero

        @pl.when(jnp.logical_not(up))
        def _():
            s[j, own + 1] = zero

    zero_halo(0)

    @pl.when(late)
    def _():
        zero_halo(2)

    @pl.when(T == 0)
    def _():
        s[1] = jnp.zeros(s.shape[1:], F32)
        m[1] = jnp.zeros(m.shape[1:], F32)

    @pl.when(T < 2)
    def _():
        m[2] = jnp.zeros(m.shape[1:], F32)

    @pl.when(T == 2)
    def _():
        s[3] = jnp.zeros(s.shape[1:], F32)

    if far:
        @pl.when(recv3)
        def _():
            zero_halo(3)

    for c in weights:
        c.wait()

    def prepare(w, left, r, mix, bias, tall):
        for a in range(3):
            for k in range(3):
                hi, lo = split(w[a, k].T)
                for i, piece in enumerate((hi, hi, lo)):
                    left[pl.ds(a * out_ch, out_ch), pl.ds((3 * k + i) * ch, ch)] = piece
        hi, lo = split(r[...])
        for i, piece in enumerate((hi, hi, lo)):
            mix[:, pl.ds(i * ch, ch)] = piece
        tall[...] = jnp.broadcast_to(bias[...], (out_ch, out_ch)).T

    prepare(w1, l1, r1, q1, b1, c1)
    acc[...] = jnp.zeros_like(acc)
    acc2[...] = jnp.zeros_like(acc2)

    @pl.when(down)
    def _():
        halo_up(0, h0s, h0r).wait_recv()

    @pl.when(up)
    def _():
        halo_down(0, h0s, h0r).wait_recv()

    @pl.when(even)
    def _():
        part(0, 0).start()
        part(0, own + 1).start()

    prepare(w2, l2, r2, q2, b2, c2)

    def push(low, high, left, pieces):
        p = jnp.dot(left[...], jnp.concatenate(pieces, axis=0), preferred_element_type=F32)
        p0, p1, p2 = p[:out_ch], p[out_ch:2 * out_ch], p[2 * out_ch:]
        n = length
        low[...] = low[...] + jnp.concatenate([p0[:, :n] + p1[:, n:], p0[:, n:]], axis=1)
        high[...] = high[...] + jnp.concatenate([p2[:, :n], p1[:, :n] + p2[:, n:]], axis=1)

    def gate(total, mix, tall, base):
        bias = tall[...]
        bias = jnp.concatenate([bias] * (total.shape[1] // bias.shape[1]), axis=1)
        pre = total + bias
        g = jnp.tanh(pre[:ch]) * (0.5 * jnp.tanh(0.5 * pre[ch:]) + 0.5)
        return base + jnp.dot(mix[...], jnp.concatenate(thirds(g), axis=0), preferred_element_type=F32)

    def straddle(ref, j, r):
        return jnp.concatenate([ref[j, r, :, length:], ref[j, r + 1, :, :length]], axis=1)

    def emit(slot, cur, r, dst):
        value = gate(acc[slot, r + 1], q1, c1, straddle(s, cur, r))
        row = F * fib + 2 * r - 1
        lo = jnp.where((row >= 0) & (row < nf * fib), value[:, :length], 0.0)
        hi = jnp.where((row + 1 >= 0) & (row + 1 < nf * fib), value[:, length:], 0.0)
        m[dst, r] = jnp.concatenate([lo, hi], axis=1)

    def first(slot, i, q, cur, prev, dst):
        chi, clo = split(s[cur, q])
        phi, plo = split(s[prev, q])
        d, n = DILATION_ONE, length

        def shift(p, c):
            return jnp.concatenate([p[:, d:n], c[:, :d], p[:, n + d:], c[:, n:n + d]], axis=1)

        shi, slo = shift(phi, chi), shift(plo, clo)
        push(acc.at[slot, q + 1], acc.at[slot, q], l1, [chi, clo, chi, shi, slo, shi, phi, plo, phi])

        @pl.when(i >= 2)
        def _():
            emit(slot, cur, jnp.where(i == wide - 1, own - 2, pick(i, emits)), dst)

    def out_emit(p):
        value = gate(acc2[p + 1], q2, c2, straddle(m, 0, p))
        for e in range(2):
            for c in range(0, length, 128):
                out_ref[pl.ds(c // 128 * fib + 2 * p + e, ch, stride=fib * length // 128), :] = value[:, e * length + c:e * length + c + 128]

    def last(i):
        r = pick(i, order2)

        @pl.when(T >= 1)
        def _():
            share(0, r).wait_recv()
        pieces = []
        for k in range(3):
            pieces += thirds(m[k, r])
        push(acc2.at[r + 1], acc2.at[r], l2, pieces)

        @pl.when(i >= 2)
        def _():
            out_emit(i - 2)

    def send_mid(r):
        @pl.when(even)
        def _():
            share(0, r).start()

        @pl.when(isodd & late)
        def _():
            share(2, r).start()

    def forward(q):
        @pl.when(even)
        def _():
            part3(q).start()

        @pl.when(isodd)
        def _():
            part(2, q).start()

    def service_top():
        cross(own).wait_recv()

        @pl.when(up)
        def _():
            halo_up(2, h2s, h2r).start()
        forward(own)

    def early(i, carry):
        q = pick(i, order)

        @pl.when(T >= 1)
        def _():
            part(0, q).wait_recv()

        @pl.when((T == 0) & (i >= 3))
        def _():
            send_mid(pick(i - 1, emits))
        first(0, i, q, 0, 1, 0)

        @pl.when(late & (i == 3))
        def _():
            service_top()
        return carry

    @pl.when(isodd | (T == 0))
    def _():
        lax.fori_loop(0, wide, early, 0)
        emit(0, 0, own - 1, 0)

        @pl.when(T == 0)
        def _():
            send_mid(own - 2)
            send_mid(own - 1)

    def stream(i, carry):
        q = pick(i, order)

        @pl.when(i >= 3)
        def _():
            send_mid(pick(i - 1, emits))

        @pl.when(i >= 4)
        def _():
            last(i - 4)

        @pl.when(even & (i == 0))
        def _():
            service_top()

        @pl.when(i == 1)
        def _():
            @pl.when(down)
            def _():
                halo_up(2, h2s, h2r).wait_recv()
            forward(q)

        @pl.when(i == 3)
        def _():
            @pl.when(up)
            def _():
                halo_down(2, h2s, h2r).wait_recv()
            forward(q)

        @pl.when((i == 2) | (i >= 4))
        def _():
            cross(q).wait_recv()

            @pl.when((i == 2) & down)
            def _():
                halo_down(2, h2s, h2r).start()
            forward(q)

        @pl.when(isodd)
        def _():
            part3(q).wait_recv()
        first(1, i, q, 2, 3, 2)

        @pl.when(even)
        def _():
            part(0, q).wait_recv()
            first(0, i, q, 0, 1, 0)
        return carry

    @pl.when(late)
    def _():
        if far:
            for i, e, _ok, ok in thirds_list:
                @pl.when(recv3 if ok is None else recv3 & ok)
                def _(i=i, e=e):
                    third(i, e).wait_recv()
        lax.fori_loop(0, wide, stream, 0)

        @pl.when(even)
        def _():
            emit(0, 0, own - 1, 0)
        emit(1, 2, own - 1, 2)
        send_mid(own - 2)
        send_mid(own - 1)

    def final(i, carry):
        last(i)
        return carry

    lax.fori_loop(jnp.where(late, wide - 4, 0), mid, final, 0)
    out_emit(own - 1)

    @pl.when(T + 2 < nt)
    def _():
        for q in arrive:
            cross(q).wait_send()

    @pl.when(up)
    def _():
        halo_up(0, h0s, h0r).wait_send()

        @pl.when(late)
        def _():
            halo_up(2, h2s, h2r).wait_send()

    @pl.when(down)
    def _():
        halo_down(0, h0s, h0r).wait_send()

        @pl.when(late)
        def _():
            halo_down(2, h2s, h2r).wait_send()

    for q in range(wide):
        @pl.when(even | late)
        def _(q=q):
            part(0, q).wait_send()

        @pl.when(even & late)
        def _(q=q):
            part3(q).wait_send()

    @pl.when(even | late)
    def _():
        for r in range(mid):
            share(0, r).wait_send()

    if far:
        for i, e, ok, _ok in thirds_list:
            @pl.when(send3 if ok is None else send3 & ok)
            def _(i=i, e=e):
                third(i, e).wait_send()


def solution(mesh):
    nt, nf = mesh.shape["tm"], mesh.shape["fibre"]
    placed = (P(None, "fibre", "tm"), P(), P(), P(), P(), P(), P())

    def body(signal, w1, b1, r1, w2, b2, r2):
        ch, fib, length = signal.shape
        assert length == DILATION_TWO == 2 * DILATION_ONE and nt % 2 == 0 and fib % 2 == 0 and fib >= 8
        x = signal.reshape(ch, fib, length // 128, 128).transpose(0, 2, 1, 3).reshape(-1, 128)
        out_ch = w1.shape[2]
        own = fib // 2
        w1, w2 = jnp.transpose(w1, (0, 1, 3, 2)), jnp.transpose(w2, (0, 1, 3, 2))
        b1 = b1.reshape(1, out_ch)
        b2 = b2.reshape(1, out_ch)
        dma = lambda n: pltpu.SemaphoreType.DMA((n,))
        out = pl.pallas_call(
            lambda *refs: kernel(nt, nf, fib, *refs),
            name="gated_layers",
            out_shape=jax.ShapeDtypeStruct(x.shape, F32),
            in_specs=[pl.BlockSpec(memory_space=pl.ANY)] * 7,
            out_specs=pl.BlockSpec(memory_space=pltpu.VMEM),
            scratch_shapes=[
                pltpu.VMEM((4, own + 2, ch, 2 * length), F32),
                pltpu.VMEM((3, own + 1, ch, 2 * length), F32),
                pltpu.VMEM(x.shape, F32),
                pltpu.VMEM(w1.shape, F32), pltpu.VMEM(b1.shape, F32), pltpu.VMEM(r1.shape, F32),
                pltpu.VMEM(w2.shape, F32), pltpu.VMEM(b2.shape, F32), pltpu.VMEM(r2.shape, F32),
                pltpu.VMEM((3 * out_ch, 9 * ch), BF), pltpu.VMEM((3 * out_ch, 9 * ch), BF),
                pltpu.VMEM((ch, 3 * ch), BF), pltpu.VMEM((ch, 3 * ch), BF),
                pltpu.VMEM((out_ch, out_ch), F32), pltpu.VMEM((out_ch, out_ch), F32),
                pltpu.VMEM((2, own + 3, out_ch, 2 * length), F32),
                pltpu.VMEM((own + 2, out_ch, 2 * length), F32),
                dma(1), dma(6), dma(2), dma(2), dma(own + 1), dma(own + 1), dma(2), dma(2),
                dma(own + 2), dma(own + 2), dma(own + 2), dma(own + 2),
                dma(own + 1), dma(own + 1), dma(3), dma(3),
            ],
            compiler_params=pltpu.CompilerParams(collective_id=0, has_side_effects=True),
        )(x, w1, b1, r1, w2, b2, r2)
        out = out.reshape(ch, length // 128, fib, 128).transpose(0, 2, 1, 3)
        return out.reshape(ch, fib, length)

    return jax.shard_map(body, mesh=mesh, in_specs=placed, out_specs=P(None, "fibre", "tm"), check_vma=False)
```

```python
import jax
import jax.numpy as jnp
from jax import lax
from jax.experimental import pallas as pl
from jax.experimental.pallas import tpu as pltpu
from jax.sharding import PartitionSpec as P

DILATION_ONE = 128
DILATION_TWO = 256
BF = jnp.bfloat16
F32 = jnp.float32


def split(value):
    hi = value.astype(BF)
    return hi, (value - hi.astype(F32)).astype(BF)


def thirds(value):
    hi, lo = split(value)
    return [hi, lo, hi]


def pick(i, values):
    out = jnp.int32(values[-1])
    for n in range(len(values) - 2, -1, -1):
        out = jnp.where(i == n, jnp.int32(values[n]), out)
    return out


def kernel(
    nt, nf, fib,
    x_hbm, w1_hbm, b1_hbm, r1_hbm, w2_hbm, b2_hbm, r2_hbm, out_ref,
    s, m, xv, w1, b1, r1, w2, b2, r2, l1, l2, q1, q2, c1, c2, acc, acc2,
    in_sem, w_sem, h0s, h0r, xs, xr, h2s, h2r, ps, pr, ts, tr, ms, mr, es, er,
):
    T = lax.axis_index("tm")
    F = lax.axis_index("fibre")
    odd = lax.rem(T, 2)
    even = odd == 0
    isodd = odd == 1
    late = T >= 2
    partner = T + 1 - 2 * odd
    ch, length = s.shape[2], s.shape[3] // 2
    own = fib // 2
    wide = own + 2
    mid = own + 1
    out_ch = 2 * ch
    far = nt > 4
    up, down = F + 1 < nf, F > 0
    arrive = [own] + list(range(1, own))
    order = [own] + list(range(own)) + [own + 1]

    def dev(t, f):
        return {"tm": t, "fibre": f}

    load = pltpu.make_async_copy(x_hbm, xv, in_sem.at[0])
    load.start()
    weights = [
        pltpu.make_async_copy(a, b, w_sem.at[i])
        for i, (a, b) in enumerate(
            [(w1_hbm, w1), (b1_hbm, b1), (r1_hbm, r1), (w2_hbm, w2), (b2_hbm, b2), (r2_hbm, r2)]
        )
    ]
    for c in weights:
        c.start()

    barrier = pltpu.get_barrier_semaphore()
    friends = [(partner, F, None), (T, F + 1, up), (T, F - 1, down), (T + 2, F, T + 2 < nt), (T - 2, F, late)]
    if far:
        send3 = isodd & (T + 3 < nt)
        recv3 = even & (T >= 4)
        for e, ok in ((0, None), (1, up), (-1, down)):
            for d, okt in ((3, send3), (-3, recv3)):
                friends.append((T + d, F + e, okt if ok is None else okt & ok))
    count = jnp.int32(0)
    for t, f, ok in friends:
        if ok is None:
            pl.semaphore_signal(barrier, inc=1, device_id=dev(t, f), device_id_type=pl.DeviceIdType.MESH)
            count = count + 1
        else:
            @pl.when(ok)
            def _(t=t, f=f):
                pl.semaphore_signal(barrier, inc=1, device_id=dev(t, f), device_id_type=pl.DeviceIdType.MESH)
            count = count + ok.astype(jnp.int32)

    load.wait()
    for f in range(fib):
        for c in range(0, length, 128):
            s[0, 1 + f // 2, :, pl.ds((f % 2) * length + c, 128)] = xv[pl.ds(c // 128 * fib + f, ch, stride=fib * length // 128), :]
    pl.semaphore_wait(barrier, count)

    def remote(src, dst, ssem, rsem, t, f):
        return pltpu.make_async_remote_copy(
            src_ref=src, dst_ref=dst, send_sem=ssem, recv_sem=rsem,
            device_id=dev(t, f), device_id_type=pl.DeviceIdType.MESH,
        )

    def halo_up(j, ss, rr):
        return remote(s.at[j, own], s.at[j, 0], ss.at[0], rr.at[0], T, F + 1)

    def halo_down(j, ss, rr):
        return remote(s.at[j, 1], s.at[j, own + 1], ss.at[1], rr.at[1], T, F - 1)

    def cross(q):
        return remote(s.at[0, q], s.at[2, q], xs.at[q], xr.at[q], T + 2, F)

    @pl.when(up)
    def _():
        halo_up(0, h0s, h0r).start()

    @pl.when(down)
    def _():
        halo_down(0, h0s, h0r).start()

    @pl.when(T + 2 < nt)
    def _():
        for q in arrive:
            cross(q).start()

    def part(src, q):
        return remote(s.at[src, q], s.at[1, q], ps.at[q], pr.at[q], partner, F)

    def part3(q):
        return remote(s.at[2, q], s.at[3, q], ts.at[q], tr.at[q], partner, F)

    def share(src, r):
        return remote(m.at[src, r], m.at[1, r], ms.at[r], mr.at[r], partner, F)

    @pl.when(even)
    def _():
        for q in range(1, own + 1):
            part(0, q).start()

    if far:
        def third(i, e):
            if e == 0:
                src, dst = s.at[0, pl.ds(1, own)], s.at[3, pl.ds(1, own)]
            elif e == 1:
                src, dst = s.at[0, own], s.at[3, 0]
            else:
                src, dst = s.at[0, 1], s.at[3, own + 1]
            return remote(src, dst, es.at[i], er.at[i], T + 3, F + e)

        thirds_list = [(0, 0, None, None), (1, 1, up, down), (2, -1, down, up)]
        for i, e, ok, _ok in thirds_list:
            @pl.when(send3 if ok is None else send3 & ok)
            def _(i=i, e=e):
                third(i, e).start()

    zero = jnp.zeros(s.shape[2:], F32)

    def zero_halo(j):
        @pl.when(jnp.logical_not(down))
        def _():
            s[j, 0] = zero

        @pl.when(jnp.logical_not(up))
        def _():
            s[j, own + 1] = zero

    zero_halo(0)

    @pl.when(late & jnp.logical_not(down))
    def _():
        s[2, 0] = zero

    @pl.when(T == 0)
    def _():
        s[1] = jnp.zeros(s.shape[1:], F32)
        m[1] = jnp.zeros(m.shape[1:], F32)

    @pl.when(T < 2)
    def _():
        m[2] = jnp.zeros(m.shape[1:], F32)

    @pl.when(T == 2)
    def _():
        s[3] = jnp.zeros(s.shape[1:], F32)

    if far:
        @pl.when(recv3)
        def _():
            zero_halo(3)

    for c in weights:
        c.wait()

    def prepare(w, left, r, mix, bias, tall):
        for a in range(3):
            for k in range(3):
                hi, lo = split(w[a, k].T)
                for i, piece in enumerate((hi, hi, lo)):
                    left[pl.ds(a * out_ch, out_ch), pl.ds((3 * k + i) * ch, ch)] = piece
        hi, lo = split(r[...])
        for i, piece in enumerate((hi, hi, lo)):
            mix[:, pl.ds(i * ch, ch)] = piece
        tall[...] = jnp.broadcast_to(bias[...], (out_ch, out_ch)).T

    prepare(w1, l1, r1, q1, b1, c1)
    acc[...] = jnp.zeros_like(acc)
    acc2[...] = jnp.zeros_like(acc2)

    @pl.when(down)
    def _():
        halo_up(0, h0s, h0r).wait_recv()

    @pl.when(up)
    def _():
        halo_down(0, h0s, h0r).wait_recv()

    @pl.when(T + 2 < nt)
    def _():
        cross(own + 1).start()

    @pl.when(even)
    def _():
        part(0, 0).start()
        part(0, own + 1).start()

    prepare(w2, l2, r2, q2, b2, c2)

    def push(low, high, left, pieces):
        p = jnp.dot(left[...], jnp.concatenate(pieces, axis=0), preferred_element_type=F32)
        p0, p1, p2 = p[:out_ch], p[out_ch:2 * out_ch], p[2 * out_ch:]
        n = length
        low[...] = low[...] + jnp.concatenate([p0[:, :n] + p1[:, n:], p0[:, n:]], axis=1)
        high[...] = high[...] + jnp.concatenate([p2[:, :n], p1[:, :n] + p2[:, n:]], axis=1)

    def gate(total, mix, tall, base):
        bias = tall[...]
        bias = jnp.concatenate([bias] * (total.shape[1] // bias.shape[1]), axis=1)
        pre = total + bias
        g = jnp.tanh(pre[:ch]) * (0.5 * jnp.tanh(0.5 * pre[ch:]) + 0.5)
        return base + jnp.dot(mix[...], jnp.concatenate(thirds(g), axis=0), preferred_element_type=F32)

    def straddle(ref, j, r):
        return jnp.concatenate([ref[j, r, :, length:], ref[j, r + 1, :, :length]], axis=1)

    def emit(slot, cur, r, dst):
        value = gate(acc[slot, r + 1], q1, c1, straddle(s, cur, r))
        row = F * fib + 2 * r - 1
        lo = jnp.where((row >= 0) & (row < nf * fib), value[:, :length], 0.0)
        hi = jnp.where((row + 1 >= 0) & (row + 1 < nf * fib), value[:, length:], 0.0)
        m[dst, r] = jnp.concatenate([lo, hi], axis=1)

    def first(slot, i, q, cur, prev, dst):
        chi, clo = split(s[cur, q])
        phi, plo = split(s[prev, q])
        d, n = DILATION_ONE, length

        def shift(p, c):
            return jnp.concatenate([p[:, d:n], c[:, :d], p[:, n + d:], c[:, n:n + d]], axis=1)

        shi, slo = shift(phi, chi), shift(plo, clo)
        push(acc.at[slot, q + 1], acc.at[slot, q], l1, [chi, clo, chi, shi, slo, shi, phi, plo, phi])

        @pl.when(i >= 2)
        def _():
            emit(slot, cur, jnp.where(i == wide - 1, own, i - 2), dst)

    def out_emit(p):
        value = gate(acc2[p + 1], q2, c2, straddle(m, 0, p))
        for e in range(2):
            for c in range(0, length, 128):
                out_ref[pl.ds(c // 128 * fib + 2 * p + e, ch, stride=fib * length // 128), :] = value[:, e * length + c:e * length + c + 128]

    def last(i):
        r = i

        @pl.when(T >= 1)
        def _():
            share(0, r).wait_recv()
        pieces = []
        for k in range(3):
            pieces += thirds(m[k, r])
        push(acc2.at[r + 1], acc2.at[r], l2, pieces)

        @pl.when(i >= 1)
        def _():
            out_emit(i - 1)

    def send_mid(r):
        @pl.when(even)
        def _():
            share(0, r).start()

        @pl.when(isodd & late)
        def _():
            share(2, r).start()

    def forward(q):
        @pl.when(even)
        def _():
            part3(q).start()

        @pl.when(isodd)
        def _():
            part(2, q).start()

    def service_top():
        cross(own).wait_recv()

        @pl.when(up)
        def _():
            halo_up(2, h2s, h2r).start()
        forward(own)

    def early(i, carry):
        q = pick(i, order)

        @pl.when(T >= 1)
        def _():
            part(0, q).wait_recv()

        @pl.when((T == 0) & (i >= 3))
        def _():
            send_mid(i - 3)
        first(0, i, q, 0, 1, 0)

        @pl.when(late & (i == 3))
        def _():
            service_top()
        return carry

    @pl.when(isodd | (T == 0))
    def _():
        lax.fori_loop(0, wide, early, 0)
        emit(0, 0, own - 1, 0)

        @pl.when(T == 0)
        def _():
            send_mid(own)
            send_mid(own - 1)

    def stream(i, carry):
        q = pick(i, order)

        @pl.when(i >= 3)
        def _():
            send_mid(i - 3)

        @pl.when(i >= 4)
        def _():
            last(i - 4)

        @pl.when(even & (i == 0))
        def _():
            service_top()

        @pl.when(i == 1)
        def _():
            @pl.when(down)
            def _():
                halo_up(2, h2s, h2r).wait_recv()
            forward(q)

        @pl.when(i >= 2)
        def _():
            cross(q).wait_recv()
            forward(q)

        @pl.when(isodd)
        def _():
            part3(q).wait_recv()
        first(1, i, q, 2, 3, 2)

        @pl.when(even)
        def _():
            part(0, q).wait_recv()
            first(0, i, q, 0, 1, 0)
        return carry

    @pl.when(late)
    def _():
        if far:
            for i, e, _ok, ok in thirds_list:
                @pl.when(recv3 if ok is None else recv3 & ok)
                def _(i=i, e=e):
                    third(i, e).wait_recv()
        lax.fori_loop(0, wide, stream, 0)

        @pl.when(even)
        def _():
            emit(0, 0, own - 1, 0)
        emit(1, 2, own - 1, 2)
        send_mid(own)
        send_mid(own - 1)

    def final(i, carry):
        last(i)
        return carry

    lax.fori_loop(jnp.where(late, wide - 4, 0), mid, final, 0)
    @pl.when(T + 2 < nt)
    def _():
        for q in arrive + [own + 1]:
            cross(q).wait_send()

    @pl.when(up)
    def _():
        halo_up(0, h0s, h0r).wait_send()

        @pl.when(late)
        def _():
            halo_up(2, h2s, h2r).wait_send()

    @pl.when(down)
    def _():
        halo_down(0, h0s, h0r).wait_send()

    for q in range(wide):
        @pl.when(even | late)
        def _(q=q):
            part(0, q).wait_send()

        @pl.when(even & late)
        def _(q=q):
            part3(q).wait_send()

    @pl.when(even | late)
    def _():
        for r in range(mid):
            share(0, r).wait_send()

    if far:
        for i, e, ok, _ok in thirds_list:
            @pl.when(send3 if ok is None else send3 & ok)
            def _(i=i, e=e):
                third(i, e).wait_send()


def solution(mesh):
    nt, nf = mesh.shape["tm"], mesh.shape["fibre"]
    placed = (P(None, "fibre", "tm"), P(), P(), P(), P(), P(), P())

    def body(signal, w1, b1, r1, w2, b2, r2):
        ch, fib, length = signal.shape
        assert length == DILATION_TWO == 2 * DILATION_ONE and nt % 2 == 0 and fib % 2 == 0 and fib >= 8
        x = signal.reshape(ch, fib, length // 128, 128).transpose(0, 2, 1, 3).reshape(-1, 128)
        out_ch = w1.shape[2]
        own = fib // 2
        w1, w2 = jnp.transpose(w1, (0, 1, 3, 2)), jnp.transpose(w2, (0, 1, 3, 2))
        b1 = b1.reshape(1, out_ch)
        b2 = b2.reshape(1, out_ch)
        dma = lambda n: pltpu.SemaphoreType.DMA((n,))
        out = pl.pallas_call(
            lambda *refs: kernel(nt, nf, fib, *refs),
            name="gated_layers",
            out_shape=jax.ShapeDtypeStruct(x.shape, F32),
            in_specs=[pl.BlockSpec(memory_space=pl.ANY)] * 7,
            out_specs=pl.BlockSpec(memory_space=pltpu.VMEM),
            scratch_shapes=[
                pltpu.VMEM((4, own + 2, ch, 2 * length), F32),
                pltpu.VMEM((3, own + 1, ch, 2 * length), F32),
                pltpu.VMEM(x.shape, F32),
                pltpu.VMEM(w1.shape, F32), pltpu.VMEM(b1.shape, F32), pltpu.VMEM(r1.shape, F32),
                pltpu.VMEM(w2.shape, F32), pltpu.VMEM(b2.shape, F32), pltpu.VMEM(r2.shape, F32),
                pltpu.VMEM((3 * out_ch, 9 * ch), BF), pltpu.VMEM((3 * out_ch, 9 * ch), BF),
                pltpu.VMEM((ch, 3 * ch), BF), pltpu.VMEM((ch, 3 * ch), BF),
                pltpu.VMEM((out_ch, out_ch), F32), pltpu.VMEM((out_ch, out_ch), F32),
                pltpu.VMEM((2, own + 3, out_ch, 2 * length), F32),
                pltpu.VMEM((own + 2, out_ch, 2 * length), F32),
                dma(1), dma(6), dma(2), dma(2), dma(own + 2), dma(own + 2), dma(2), dma(2),
                dma(own + 2), dma(own + 2), dma(own + 2), dma(own + 2),
                dma(own + 1), dma(own + 1), dma(3), dma(3),
            ],
            compiler_params=pltpu.CompilerParams(collective_id=0, has_side_effects=True),
        )(x, w1, b1, r1, w2, b2, r2)
        out = out.reshape(ch, length // 128, fib, 128).transpose(0, 2, 1, 3)
        return out.reshape(ch, fib, length)

    return jax.shard_map(body, mesh=mesh, in_specs=placed, out_specs=P(None, "fibre", "tm"), check_vma=False)
```

```python
import jax
import jax.numpy as jnp
from jax import lax
from jax.experimental import pallas as pl
from jax.experimental.pallas import tpu as pltpu
from jax.sharding import PartitionSpec as P

DILATION_ONE = 128
DILATION_TWO = 256
BF = jnp.bfloat16
F32 = jnp.float32


def split(value):
    hi = value.astype(BF)
    return hi, (value - hi.astype(F32)).astype(BF)


def thirds(value):
    hi, lo = split(value)
    return [hi, lo, hi]


def pick(i, values):
    out = jnp.int32(values[-1])
    for n in range(len(values) - 2, -1, -1):
        out = jnp.where(i == n, jnp.int32(values[n]), out)
    return out


def kernel(
    nt, nf, fib,
    x_hbm, w1_hbm, b1_hbm, r1_hbm, w2_hbm, b2_hbm, r2_hbm, out_ref,
    s, m, xv, w1, b1, r1, w2, b2, r2, l1, l2, q1, q2, c1, c2, acc, acc2,
    in_sem, w_sem, h0s, h0r, xs, xr, ps, pr, ts, tr, ms, mr, es, er,
):
    T = lax.axis_index("tm")
    F = lax.axis_index("fibre")
    odd = lax.rem(T, 2)
    even = odd == 0
    isodd = odd == 1
    late = T >= 2
    partner = T + 1 - 2 * odd
    ch, length = s.shape[2], s.shape[3] // 2
    own = fib // 2
    wide = own + 2
    mid = own + 1
    out_ch = 2 * ch
    far = nt > 4
    up, down = F + 1 < nf, F > 0
    arrive = list(range(1, own + 1))
    order = arrive + [0, own + 1]
    order2 = list(range(1, own)) + [0, own]

    def dev(t, f):
        return {"tm": t, "fibre": f}

    load = pltpu.make_async_copy(x_hbm, xv, in_sem.at[0])
    load.start()
    weights = [
        pltpu.make_async_copy(a, b, w_sem.at[i])
        for i, (a, b) in enumerate(
            [(w1_hbm, w1), (b1_hbm, b1), (r1_hbm, r1), (w2_hbm, w2), (b2_hbm, b2), (r2_hbm, r2)]
        )
    ]
    for c in weights:
        c.start()

    barrier = pltpu.get_barrier_semaphore()
    friends = [(partner, F, None), (T, F + 1, up), (T, F - 1, down), (T + 2, F, T + 2 < nt), (T - 2, F, late)]
    if far:
        send3 = isodd & (T + 3 < nt)
        recv3 = even & (T >= 4)
        for e, ok in ((0, None), (1, up), (-1, down)):
            for d, okt in ((3, send3), (-3, recv3)):
                friends.append((T + d, F + e, okt if ok is None else okt & ok))
    count = jnp.int32(0)
    for t, f, ok in friends:
        if ok is None:
            pl.semaphore_signal(barrier, inc=1, device_id=dev(t, f), device_id_type=pl.DeviceIdType.MESH)
            count = count + 1
        else:
            @pl.when(ok)
            def _(t=t, f=f):
                pl.semaphore_signal(barrier, inc=1, device_id=dev(t, f), device_id_type=pl.DeviceIdType.MESH)
            count = count + ok.astype(jnp.int32)

    load.wait()
    for f in range(fib):
        for c in range(0, length, 128):
            s[0, 1 + f // 2, :, pl.ds((f % 2) * length + c, 128)] = xv[pl.ds(c // 128 * fib + f, ch, stride=fib * length // 128), :]
    pl.semaphore_wait(barrier, count)

    def remote(src, dst, ssem, rsem, t, f):
        return pltpu.make_async_remote_copy(
            src_ref=src, dst_ref=dst, send_sem=ssem, recv_sem=rsem,
            device_id=dev(t, f), device_id_type=pl.DeviceIdType.MESH,
        )

    def halo_up(j, ss, rr):
        return remote(s.at[j, own], s.at[j, 0], ss.at[0], rr.at[0], T, F + 1)

    def halo_down(j, ss, rr):
        return remote(s.at[j, 1], s.at[j, own + 1], ss.at[1], rr.at[1], T, F - 1)

    def cross(q):
        return remote(s.at[0, q], s.at[2, q], xs.at[q], xr.at[q], T + 2, F)

    @pl.when(up)
    def _():
        halo_up(0, h0s, h0r).start()

    @pl.when(down)
    def _():
        halo_down(0, h0s, h0r).start()

    @pl.when(T + 2 < nt)
    def _():
        for q in arrive:
            cross(q).start()

    def part(src, q):
        return remote(s.at[src, q], s.at[1, q], ps.at[q], pr.at[q], partner, F)

    def part3(q):
        return remote(s.at[2, q], s.at[3, q], ts.at[q], tr.at[q], partner, F)

    def share(src, r):
        return remote(m.at[src, r], m.at[1, r], ms.at[r], mr.at[r], partner, F)

    @pl.when(even)
    def _():
        for q in range(1, own + 1):
            part(0, q).start()

    if far:
        def third(i, e):
            if e == 0:
                src, dst = s.at[0, pl.ds(1, own)], s.at[3, pl.ds(1, own)]
            elif e == 1:
                src, dst = s.at[0, own], s.at[3, 0]
            else:
                src, dst = s.at[0, 1], s.at[3, own + 1]
            return remote(src, dst, es.at[i], er.at[i], T + 3, F + e)

        thirds_list = [(0, 0, None, None), (1, 1, up, down), (2, -1, down, up)]
        for i, e, ok, _ok in thirds_list:
            @pl.when(send3 if ok is None else send3 & ok)
            def _(i=i, e=e):
                third(i, e).start()

    zero = jnp.zeros(s.shape[2:], F32)

    def zero_halo(j):
        @pl.when(jnp.logical_not(down))
        def _():
            s[j, 0] = zero

        @pl.when(jnp.logical_not(up))
        def _():
            s[j, own + 1] = zero

    zero_halo(0)


    @pl.when(T == 0)
    def _():
        s[1] = jnp.zeros(s.shape[1:], F32)
        m[1] = jnp.zeros(m.shape[1:], F32)

    @pl.when(T < 2)
    def _():
        m[2] = jnp.zeros(m.shape[1:], F32)

    @pl.when(T == 2)
    def _():
        s[3] = jnp.zeros(s.shape[1:], F32)

    if far:
        @pl.when(recv3)
        def _():
            zero_halo(3)

    for c in weights:
        c.wait()

    def prepare(w, left, r, mix, bias, tall):
        for a in range(3):
            for k in range(3):
                hi, lo = split(w[a, k].T)
                for i, piece in enumerate((hi, hi, lo)):
                    left[pl.ds(a * out_ch, out_ch), pl.ds((3 * k + i) * ch, ch)] = piece
        hi, lo = split(r[...])
        for i, piece in enumerate((hi, hi, lo)):
            mix[:, pl.ds(i * ch, ch)] = piece
        tall[...] = jnp.broadcast_to(bias[...], (out_ch, out_ch)).T

    prepare(w1, l1, r1, q1, b1, c1)
    acc[...] = jnp.zeros_like(acc)
    acc2[...] = jnp.zeros_like(acc2)

    @pl.when(down)
    def _():
        halo_up(0, h0s, h0r).wait_recv()

    @pl.when(up)
    def _():
        halo_down(0, h0s, h0r).wait_recv()

    @pl.when(T + 2 < nt)
    def _():
        cross(0).start()
        cross(own + 1).start()

    @pl.when(even)
    def _():
        part(0, 0).start()
        part(0, own + 1).start()

    prepare(w2, l2, r2, q2, b2, c2)

    def push(low, high, left, pieces):
        p = jnp.dot(left[...], jnp.concatenate(pieces, axis=0), preferred_element_type=F32)
        p0, p1, p2 = p[:out_ch], p[out_ch:2 * out_ch], p[2 * out_ch:]
        n = length
        low[...] = low[...] + jnp.concatenate([p0[:, :n] + p1[:, n:], p0[:, n:]], axis=1)
        high[...] = high[...] + jnp.concatenate([p2[:, :n], p1[:, :n] + p2[:, n:]], axis=1)

    def gate(total, mix, tall, base):
        bias = tall[...]
        bias = jnp.concatenate([bias] * (total.shape[1] // bias.shape[1]), axis=1)
        pre = total + bias
        g = jnp.tanh(pre[:ch]) * (0.5 * jnp.tanh(0.5 * pre[ch:]) + 0.5)
        return base + jnp.dot(mix[...], jnp.concatenate(thirds(g), axis=0), preferred_element_type=F32)

    def straddle(ref, j, r):
        return jnp.concatenate([ref[j, r, :, length:], ref[j, r + 1, :, :length]], axis=1)

    def ready(i):
        return jnp.where(i < own, i, jnp.where(i == own, 0, own))

    def emit(slot, cur, r, dst):
        value = gate(acc[slot, r + 1], q1, c1, straddle(s, cur, r))
        row = F * fib + 2 * r - 1
        lo = jnp.where((row >= 0) & (row < nf * fib), value[:, :length], 0.0)
        hi = jnp.where((row + 1 >= 0) & (row + 1 < nf * fib), value[:, length:], 0.0)
        m[dst, r] = jnp.concatenate([lo, hi], axis=1)

    def first(slot, i, q, cur, prev, dst):
        chi, clo = split(s[cur, q])
        phi, plo = split(s[prev, q])
        d, n = DILATION_ONE, length

        def shift(p, c):
            return jnp.concatenate([p[:, d:n], c[:, :d], p[:, n + d:], c[:, n:n + d]], axis=1)

        shi, slo = shift(phi, chi), shift(plo, clo)
        push(acc.at[slot, q + 1], acc.at[slot, q], l1, [chi, clo, chi, shi, slo, shi, phi, plo, phi])

        @pl.when(i >= 1)
        def _():
            emit(slot, cur, ready(i), dst)

    def out_emit(p):
        value = gate(acc2[p + 1], q2, c2, straddle(m, 0, p))
        for e in range(2):
            for c in range(0, length, 128):
                out_ref[pl.ds(c // 128 * fib + 2 * p + e, ch, stride=fib * length // 128), :] = value[:, e * length + c:e * length + c + 128]

    def last(i):
        r = pick(i, order2)

        @pl.when(T >= 1)
        def _():
            share(0, r).wait_recv()
        pieces = []
        for k in range(3):
            pieces += thirds(m[k, r])
        push(acc2.at[r + 1], acc2.at[r], l2, pieces)

        @pl.when(i >= 1)
        def _():
            out_emit(jnp.where(i < own - 1, i, jnp.where(i == own - 1, 0, own - 1)))

    def send_mid(r):
        @pl.when(even)
        def _():
            share(0, r).start()

        @pl.when(isodd & late)
        def _():
            share(2, r).start()

    def forward(q):
        @pl.when(even)
        def _():
            part3(q).start()

        @pl.when(isodd)
        def _():
            part(2, q).start()

    def early(i, carry):
        q = pick(i, order)

        @pl.when(T >= 1)
        def _():
            part(0, q).wait_recv()

        @pl.when((T == 0) & (i >= 2))
        def _():
            send_mid(ready(i - 1))
        first(0, i, q, 0, 1, 0)

        return carry

    @pl.when(isodd | (T == 0))
    def _():
        lax.fori_loop(0, wide, early, 0)

        @pl.when(T == 0)
        def _():
            send_mid(own)

    def stream(i, carry):
        q = pick(i, order)

        @pl.when(i >= 2)
        def _():
            send_mid(ready(i - 1))

        @pl.when(i >= 3)
        def _():
            last(i - 3)

        cross(q).wait_recv()
        forward(q)

        @pl.when(isodd)
        def _():
            part3(q).wait_recv()
        first(1, i, q, 2, 3, 2)

        @pl.when(even)
        def _():
            part(0, q).wait_recv()
            first(0, i, q, 0, 1, 0)
        return carry

    @pl.when(late)
    def _():
        if far:
            for i, e, _ok, ok in thirds_list:
                @pl.when(recv3 if ok is None else recv3 & ok)
                def _(i=i, e=e):
                    third(i, e).wait_recv()
        lax.fori_loop(0, wide, stream, 0)
        send_mid(own)

    def final(i, carry):
        last(i)
        return carry

    lax.fori_loop(jnp.where(late, wide - 3, 0), mid, final, 0)
    @pl.when(T + 2 < nt)
    def _():
        for q in order:
            cross(q).wait_send()

    @pl.when(up)
    def _():
        halo_up(0, h0s, h0r).wait_send()

    @pl.when(down)
    def _():
        halo_down(0, h0s, h0r).wait_send()

    for q in range(wide):
        @pl.when(even | late)
        def _(q=q):
            part(0, q).wait_send()

        @pl.when(even & late)
        def _(q=q):
            part3(q).wait_send()

    @pl.when(even | late)
    def _():
        for r in range(mid):
            share(0, r).wait_send()

    if far:
        for i, e, ok, _ok in thirds_list:
            @pl.when(send3 if ok is None else send3 & ok)
            def _(i=i, e=e):
                third(i, e).wait_send()


def solution(mesh):
    nt, nf = mesh.shape["tm"], mesh.shape["fibre"]
    placed = (P(None, "fibre", "tm"), P(), P(), P(), P(), P(), P())

    def body(signal, w1, b1, r1, w2, b2, r2):
        ch, fib, length = signal.shape
        assert length == DILATION_TWO == 2 * DILATION_ONE and nt % 2 == 0 and fib % 2 == 0 and fib >= 8
        x = signal.reshape(ch, fib, length // 128, 128).transpose(0, 2, 1, 3).reshape(-1, 128)
        out_ch = w1.shape[2]
        own = fib // 2
        w1, w2 = jnp.transpose(w1, (0, 1, 3, 2)), jnp.transpose(w2, (0, 1, 3, 2))
        b1 = b1.reshape(1, out_ch)
        b2 = b2.reshape(1, out_ch)
        dma = lambda n: pltpu.SemaphoreType.DMA((n,))
        out = pl.pallas_call(
            lambda *refs: kernel(nt, nf, fib, *refs),
            name="gated_layers",
            out_shape=jax.ShapeDtypeStruct(x.shape, F32),
            in_specs=[pl.BlockSpec(memory_space=pl.ANY)] * 7,
            out_specs=pl.BlockSpec(memory_space=pltpu.VMEM),
            scratch_shapes=[
                pltpu.VMEM((4, own + 2, ch, 2 * length), F32),
                pltpu.VMEM((3, own + 1, ch, 2 * length), F32),
                pltpu.VMEM(x.shape, F32),
                pltpu.VMEM(w1.shape, F32), pltpu.VMEM(b1.shape, F32), pltpu.VMEM(r1.shape, F32),
                pltpu.VMEM(w2.shape, F32), pltpu.VMEM(b2.shape, F32), pltpu.VMEM(r2.shape, F32),
                pltpu.VMEM((3 * out_ch, 9 * ch), BF), pltpu.VMEM((3 * out_ch, 9 * ch), BF),
                pltpu.VMEM((ch, 3 * ch), BF), pltpu.VMEM((ch, 3 * ch), BF),
                pltpu.VMEM((out_ch, out_ch), F32), pltpu.VMEM((out_ch, out_ch), F32),
                pltpu.VMEM((2, own + 3, out_ch, 2 * length), F32),
                pltpu.VMEM((own + 2, out_ch, 2 * length), F32),
                dma(1), dma(6), dma(2), dma(2), dma(own + 2), dma(own + 2),
                dma(own + 2), dma(own + 2), dma(own + 2), dma(own + 2),
                dma(own + 1), dma(own + 1), dma(3), dma(3),
            ],
            compiler_params=pltpu.CompilerParams(collective_id=0, has_side_effects=True),
        )(x, w1, b1, r1, w2, b2, r2)
        out = out.reshape(ch, length // 128, fib, 128).transpose(0, 2, 1, 3)
        return out.reshape(ch, fib, length)

    return jax.shard_map(body, mesh=mesh, in_specs=placed, out_specs=P(None, "fibre", "tm"), check_vma=False)
```
